768 devices in a mesh: dp: 12 (over z_lo, core), tensor: 8 (over z_hi, x), pipe: 8 (over y).
Axes of the slice: x: 4, y: 8, z: 12 (z_hi: 2, z_lo: 6; z = z_hi * 6 + z_lo), core: 2. Of those that a mesh axis runs over, the one named last changes fastest.
Arguments:
- attn_policy: bfloat16 [12, 1024, 4608], P('dp', 'pipe', 'tensor'), may hold values from -0.046875 to 0.046875
- attn_frozen: bfloat16 [12, 1024, 4608], P('dp', 'pipe', 'tensor'), may hold values from -0.046875 to 0.046875
- readout: bfloat16 [12, 1024, 8192], P('dp', 'pipe'), may hold values from -6 to 6
- rest_policy: float32 [12, 1024], P('dp', 'pipe'), may hold values from -3 to 3
- rest_frozen: float32 [12, 1024], P('dp', 'pipe'), may hold values from -3 to 3
- policy_out: bfloat16 [4608, 8192], P('tensor'), may hold values from -0.0625 to 0.0625
- frozen_out: bfloat16 [4608, 8192], P(('tensor', 'dp', 'pipe')), may hold values from -0.0625 to 0.0625
- rewards: float32 [12], replicated, may hold values from -4 to 4
- group_ids: int32 [12], replicated, may hold values from 0 to 5
- prompt_len: int32 [12], replicated, may hold values from 1 to 255
- response_len: int32 [12], replicated, may hold values from 256 to 768
Outputs:
- upstream_grad: bfloat16 [12, 1024, 4608], P('dp', 'pipe', 'tensor')
The draws below stay inside these ranges and needn't reach their ends.
Inputs may be any that keep to these rules, and one draw needn't show every extreme that they name: `prompt_len`: prompt and response together fit in a rollout.
All inputs are finite; a program needn't handle non-finite values.
Results may differ from the reference program's by a relative error of at most 0.001.
Values may be sent and summed in bfloat16 or wider, within the bound.
No kernel may reach another device: no remote copies, remote signals or barrier semaphores. Data moves between devices by JAX's collectives and lax.ppermute only.
A program may use at most 128 MiB of HBM per device.

```python
import jax
import jax.numpy as jnp
from jax import lax

D = 8192
TOK_DEV = 128
QDIM = 4608
SEQ = 1024
NSEQ = 12
GROUPS = 6


def with_ends(entries, rng, low, largest):
    index_at = [jax.random.randint(jax.random.fold_in(rng, axis), (), 0, length) for axis, length in enumerate(entries.shape)]
    longest = entries.shape.index(max(entries.shape))
    next_to = index_at[:longest] + [(index_at[longest] + 1) % entries.shape[longest]] + index_at[longest + 1:]
    return entries.at[tuple(index_at)].set(low).at[tuple(next_to)].set(largest)


def block_levels(rng, extent, cuts, least, top_value):
    def one(axis_at, blocks):
        steps = jax.random.uniform(jax.random.fold_in(jax.random.fold_in(rng, 6), axis_at), (blocks,), jnp.float32, least / len(cuts), top_value / len(cuts))
        return jnp.repeat(jnp.exp(steps), extent[axis_at] // blocks).reshape((-1,) + (1,) * (len(extent) - axis_at - 1))

    loudness = one(*cuts[0])
    for cut in cuts[1:]:
        loudness = loudness * one(*cut)
    return loudness


def scatter_about(key, dims, spread, limit, split=(), kind=jnp.bfloat16):
    level = block_levels(key, dims, split, -0.22, 0.18) if split else 1.0
    values = jax.random.normal(key, dims, jnp.float32) * spread * level
    return jnp.minimum(jnp.maximum(values, -limit), limit).astype(kind)


def setup_inputs(seed: int = 0) -> dict:
    key_of = jax.random.split(jax.random.key(seed), 12)
    attn_policy = scatter_about(key_of[0], (NSEQ, SEQ, QDIM), (QDIM * 4) ** -0.5, 0.046875, ((0, 12), (1, 8), (2, 8)))
    attn_frozen = scatter_about(key_of[1], (NSEQ, SEQ, QDIM), (QDIM * 4) ** -0.5, 0.046875, ((0, 12), (1, 8), (2, 8)))
    readout = scatter_about(key_of[2], (NSEQ, SEQ, D), 1.0, 6.0, ((0, 12), (1, 8)))
    rest_policy = scatter_about(key_of[3], (NSEQ, SEQ), 0.5, 3.0, ((0, 12), (1, 8)), jnp.float32)
    rest_frozen = scatter_about(key_of[4], (NSEQ, SEQ), 0.5, 3.0, ((0, 12), (1, 8)), jnp.float32)
    policy_out = scatter_about(key_of[5], (QDIM, D), D ** -0.5, 0.0625, ((0, 8),))
    frozen_out = scatter_about(key_of[6], (QDIM, D), D ** -0.5, 0.0625, ((0, 768),))
    rewards = scatter_about(key_of[7], (NSEQ,), 1.0, 4.0, (), jnp.float32)
    group_ids = with_ends(jax.random.randint(key_of[8], (NSEQ,), 0, GROUPS), jax.random.fold_in(key_of[8], 1), 0, GROUPS - 1).astype(jnp.int32)
    prompt_len = with_ends(jax.random.randint(key_of[9], (NSEQ,), 1, SEQ // 4), jax.random.fold_in(key_of[9], 1), 1, (SEQ // 4) - 1).astype(jnp.int32)
    response_len = with_ends(jax.random.randint(key_of[10], (NSEQ,), SEQ // 4, 3 * SEQ // 4 + 1), jax.random.fold_in(key_of[10], 1), SEQ // 4, (3 * SEQ // 4 + 1) - 1).astype(jnp.int32)
    return {"attn_policy": attn_policy, "attn_frozen": attn_frozen, "readout": readout, "rest_policy": rest_policy, "rest_frozen": rest_frozen, "policy_out": policy_out, "frozen_out": frozen_out, "rewards": rewards, "group_ids": group_ids, "prompt_len": prompt_len, "response_len": response_len}


KL_WEIGHT = 0.1


def reference(attn_policy, attn_frozen, readout, rest_policy, rest_frozen, policy_out, frozen_out, rewards, group_ids, prompt_len, response_len):
    same_group = (group_ids[:, None] == group_ids[None, :]).astype(jnp.float32)
    group_mean = jnp.dot(same_group, rewards, precision=lax.Precision.HIGHEST) / jnp.sum(same_group, axis=1)
    advantage = rewards - group_mean
    positions = jnp.arange(SEQ, dtype=jnp.int32)

    def per_sequence(items):
        att_policy, att_frozen, unembed, base_policy, base_frozen, adv_one, start_one, length_one = items
        view_policy = jnp.dot(unembed, policy_out.T, preferred_element_type=jnp.float32)
        view_frozen = jnp.dot(unembed, frozen_out.T, preferred_element_type=jnp.float32)
        logp_policy = base_policy + jnp.sum(att_policy.astype(jnp.float32) * view_policy, axis=1)
        logp_frozen = base_frozen + jnp.sum(att_frozen.astype(jnp.float32) * view_frozen, axis=1)
        inside = (positions >= start_one) & (positions < start_one + length_one)
        weighting = jnp.where(inside, SEQ / length_one.astype(jnp.float32), 0.0)
        log_ratio = logp_frozen - logp_policy
        slope = weighting * (KL_WEIGHT * (1.0 - jnp.exp(log_ratio)) - adv_one)
        return (slope[:, None] * view_policy).astype(jnp.bfloat16)

    grads = lax.map(per_sequence, (attn_policy, attn_frozen, readout, rest_policy, rest_frozen, advantage, prompt_len, response_len))
    return jnp.roll(grads, -TOK_DEV, axis=1)
```

```python
import jax
import jax.numpy as jnp
from jax import lax
from jax.sharding import PartitionSpec as P

KL_WEIGHT = 0.1
AXES = ("dp", "tensor", "pipe")
CORES = 2
SUB = 4


def make(mesh):
    n_dp, n_tensor, n_pipe = (mesh.shape[a] for a in AXES)
    n_z = n_dp // CORES
    chunks = 2

    def flat(d, t, p):
        return (d * n_tensor + t) * n_pipe + p

    every = [(d, t, p) for d in range(n_dp) for t in range(n_tensor) for p in range(n_pipe)]
    to_partner = [(flat(d, t, p), flat(d ^ 1, t, p)) for d, t, p in every]
    along = [[z * CORES + c for z in range(n_z)] for c in range(CORES)]
    heads = [[(z * CORES + c) * n_tensor + t for c in range(CORES) for t in range(n_tensor)] for z in range(n_z)]

    def partner(array):
        return lax.ppermute(array, AXES, to_partner)

    def shift(array, by):
        return lax.ppermute(array, "pipe", [(i, (i + by) % n_pipe) for i in range(n_pipe)])

    def shards(
        attn_policy,
        attn_frozen,
        readout,
        rest_policy,
        rest_frozen,
        policy_out,
        frozen_out,
        rewards,
        group_ids,
        prompt_len,
        response_len,
    ):
        unembed = readout[0]
        tokens, width = unembed.shape
        rows = frozen_out.shape[0]
        step = width // (chunks * SUB)
        core = lax.axis_index("dp") % CORES
        section = lax.axis_index("pipe")

        units = frozen_out.reshape(rows, chunks, SUB, step).transpose(1, 2, 0, 3)
        blocks = []
        for j in range(chunks):
            unit = units[j].reshape(SUB * rows, step)
            spread = jnp.broadcast_to(unit[None], (n_z, SUB * rows, step))
            got = lax.all_to_all(spread, "dp", 0, 0, axis_index_groups=along, tiled=True)
            blocks.append(got.reshape(n_z * SUB * rows, step))

        both = jnp.concatenate([unembed, partner(unembed)], axis=0)
        seen = both.reshape(CORES * tokens, chunks, SUB, step).transpose(1, 2, 0, 3)
        seen = [seen[j].reshape(SUB * CORES * tokens, step) for j in range(chunks)]
        feats = attn_frozen[0].T.reshape(n_z, CORES, n_pipe * rows, tokens)
        mine = lax.dynamic_index_in_dim(feats, core, 1, keepdims=False)
        theirs = lax.dynamic_index_in_dim(feats, 1 - core, 1, keepdims=False)
        feats = jnp.concatenate([mine, partner(theirs)], axis=2).reshape(n_z * n_pipe * rows, CORES * tokens)
        count = n_pipe * n_z * SUB * rows
        out_row = jnp.arange(count, dtype=jnp.int32)
        r = out_row % rows
        z = out_row // (rows * SUB) % n_z
        y = out_row // (rows * SUB * n_z)
        source = (z * n_pipe + y) * rows + r
        pick = (source[:, None] == jnp.arange(n_z * n_pipe * rows, dtype=jnp.int32)[None, :]).astype(jnp.bfloat16)
        spread_feats = jnp.dot(pick, feats, preferred_element_type=jnp.float32).astype(jnp.bfloat16)
        spread_feats = spread_feats.reshape(n_pipe, n_z * SUB * rows, CORES * tokens)
        sub_of_row = jnp.arange(n_z * SUB * rows, dtype=jnp.int32) // rows % SUB
        same_sub = sub_of_row[:, None] == jnp.arange(SUB, dtype=jnp.int32)[None, :]

        def partial(block, j, hop):
            view = jnp.dot(block, seen[j].T, preferred_element_type=jnp.float32)
            view = view.reshape(n_z * SUB * rows, SUB, CORES * tokens)
            at = lax.dynamic_index_in_dim(spread_feats, (section - hop) % n_pipe, 0, keepdims=False)
            terms = jnp.where(same_sub[:, :, None], view * at.astype(jnp.float32)[:, None, :], 0.0)
            return jnp.sum(terms, axis=(0, 1))

        view_policy = jnp.dot(policy_out, unembed.T, preferred_element_type=jnp.float32)
        part_policy = jnp.sum(attn_policy[0].T.astype(jnp.float32) * view_policy, axis=0)

        half = n_pipe // 2
        parts = []
        up, down = list(blocks), list(blocks)
        for j in range(chunks):
            parts.append(partial(blocks[j], j, 0))
        for hop in range(1, half):
            for j in range(chunks):
                up[j] = shift(up[j], 1)
                down[j] = shift(down[j], -1)
            for j in range(chunks):
                parts.append(partial(up[j], j, hop))
                parts.append(partial(down[j], j, -hop))
        for j in range(chunks):
            last = shift(up[j], 1) if j % 2 == 0 else shift(down[j], -1)
            parts.append(partial(last, j, half))
        total = sum(parts)

        own, other = total[:tokens], total[tokens:]
        zero = jnp.zeros_like(own)
        same = jnp.stack([own, part_policy])
        cross = jnp.stack([other, zero])
        by_core = jnp.where(core == 0, jnp.stack([same, cross]), jnp.stack([cross, same]))
        sent = jnp.broadcast_to(by_core[:, None], (CORES, n_tensor, 2, tokens)).reshape(CORES * n_tensor, 2, tokens)
        gathered = lax.all_to_all(sent, ("dp", "tensor"), 0, 0, axis_index_groups=heads, tiled=True)
        summed = gathered.sum(axis=0)
        logp_frozen = rest_frozen[0] + summed[0]
        logp_policy = rest_policy[0] + summed[1]

        same_group = (group_ids[:, None] == group_ids[None, :]).astype(jnp.float32)
        group_mean = jnp.dot(same_group, rewards, precision=lax.Precision.HIGHEST) / jnp.sum(same_group, axis=1)
        advantage = rewards - group_mean
        chosen = jnp.arange(rewards.shape[0], dtype=jnp.int32) == lax.axis_index("dp")
        adv_one = jnp.sum(jnp.where(chosen, advantage, 0.0))
        start_one = jnp.sum(jnp.where(chosen, prompt_len, 0))
        length_one = jnp.sum(jnp.where(chosen, response_len, 0))
        seq_total = tokens * n_pipe
        positions = section * tokens + jnp.arange(tokens, dtype=jnp.int32)
        inside = (positions >= start_one) & (positions < start_one + length_one)
        weighting = jnp.where(inside, seq_total / length_one.astype(jnp.float32), 0.0)
        slope = weighting * (KL_WEIGHT * (1.0 - jnp.exp(logp_frozen - logp_policy)) - adv_one)
        token_grad = (slope[None, :] * view_policy).astype(jnp.bfloat16)
        return shift(token_grad, -1).T[None]

    return shards


def solution(mesh):
    placed = (
        P("dp", "pipe", "tensor"),
        P("dp", "pipe", "tensor"),
        P("dp", "pipe", None),
        P("dp", "pipe"),
        P("dp", "pipe"),
        P("tensor", None),
        P(("tensor", "dp", "pipe"), None),
        P(),
        P(),
        P(),
        P(),
    )
    return jax.shard_map(
        make(mesh), mesh=mesh, in_specs=placed, out_specs=P("dp", "pipe", "tensor"), check_vma=False
    )
```

```python
import jax
import jax.numpy as jnp
from jax import lax
from jax.experimental import pallas as pl
from jax.experimental.pallas import tpu as pltpu
from jax.sharding import PartitionSpec as P

KL_WEIGHT = 0.1
AXES = ("dp", "tensor", "pipe")
CORES = 2
SUB = 4
VMEM_BYTES = 16 * 1024 * 1024


def block_sums(items, own, other, sub_mask):
    count = len(items)
    half, width = own.shape
    tokens = CORES * half
    step = width // SUB

    def kernel(*refs):
        mask_ref, own_ref, other_ref, out_ref = refs[2 * count :]
        columns = jnp.concatenate([own_ref[...], other_ref[...]], axis=0)
        rows = jnp.concatenate([r[...] for r in refs[:count]], axis=0)
        view = lax.dot_general(rows, columns, (((1,), (1,)), ((), ())), preferred_element_type=jnp.float32)
        total = jnp.zeros((1, tokens), jnp.float32)
        lo = 0
        for feat_ref in refs[count : 2 * count]:
            n = feat_ref.shape[0]
            kept = feat_ref[...].astype(jnp.float32) * mask_ref[0, :n, :].astype(jnp.float32)
            total += jnp.sum(view[lo : lo + n] * kept, axis=0, keepdims=True)
            lo += n

        @pl.when(pl.program_id(0) == 0)
        def _():
            out_ref[...] = total

        @pl.when(pl.program_id(0) > 0)
        def _():
            out_ref[...] += total

    def whole(array):
        return pl.BlockSpec(array.shape, lambda k: (0, 0))

    most = max(r.shape[0] for r, _ in items)
    rows = sum(r.shape[0] for r, _ in items)
    flat = [r for r, _ in items] + [f for _, f in items]
    specs = [whole(x) for x in flat]
    specs += [
        pl.BlockSpec((1, most, tokens), lambda k: (k, 0, 0)),
        pl.BlockSpec((half, step), lambda k: (0, k)),
        pl.BlockSpec((half, step), lambda k: (0, k)),
    ]
    return pl.pallas_call(
        kernel,
        grid=(SUB,),
        out_shape=jax.ShapeDtypeStruct((1, tokens), jnp.float32),
        in_specs=specs,
        out_specs=pl.BlockSpec((1, tokens), lambda k: (0, 0)),
        cost_estimate=pl.CostEstimate(
            flops=2 * rows * width * tokens, bytes_accessed=rows * step * 2 + 4 * own.size, transcendentals=0
        ),
        compiler_params=pltpu.CompilerParams(
            dimension_semantics=("arbitrary",), vmem_limit_bytes=VMEM_BYTES
        ),
    )(*flat, sub_mask, own, other)


def make(mesh):
    n_dp, n_tensor, n_pipe = (mesh.shape[a] for a in AXES)
    n_z = n_dp // CORES
    half = n_pipe // 2

    def flat(d, t, p):
        return (d * n_tensor + t) * n_pipe + p

    every = [(d, t, p) for d in range(n_dp) for t in range(n_tensor) for p in range(n_pipe)]
    to_partner = [(flat(d, t, p), flat(d ^ 1, t, p)) for d, t, p in every]
    along = [[z * CORES + c for z in range(n_z)] for c in range(CORES)]
    heads = [[(z * CORES + c) * n_tensor + t for c in range(CORES) for t in range(n_tensor)] for z in range(n_z)]

    def partner(array):
        return lax.ppermute(array, AXES, to_partner)

    def shift(array, by):
        return lax.ppermute(array, "pipe", [(i, (i + by) % n_pipe) for i in range(n_pipe)])

    def shards(
        attn_policy,
        attn_frozen,
        readout,
        rest_policy,
        rest_frozen,
        policy_out,
        frozen_out,
        rewards,
        group_ids,
        prompt_len,
        response_len,
    ):
        own = readout[0]
        tokens, width = own.shape
        rows = frozen_out.shape[0]
        step = width // SUB
        core = lax.axis_index("dp") % CORES
        section = lax.axis_index("pipe")
        unit_rows = SUB * rows

        unit = frozen_out.reshape(rows, SUB, step).transpose(1, 0, 2).reshape(unit_rows, step)
        spread = jnp.broadcast_to(unit[None], (n_z, unit_rows, step))
        got_z = lax.all_to_all(spread, "dp", 0, 0, axis_index_groups=along, tiled=True)
        other = partner(own)
        feats = attn_frozen[0].T.reshape(n_z, CORES, n_pipe * rows, tokens)
        mine = lax.dynamic_index_in_dim(feats, core, 1, keepdims=False)
        theirs = lax.dynamic_index_in_dim(feats, 1 - core, 1, keepdims=False)
        theirs = partner(theirs)
        feats = jnp.concatenate([mine, theirs], axis=2).reshape(n_z * n_pipe * rows, CORES * tokens)

        def features(z, y, r):
            source = (z * n_pipe + y) * rows + r
            columns = jnp.arange(n_z * n_pipe * rows, dtype=jnp.int32)
            pick = (source[:, None] == columns[None, :]).astype(jnp.bfloat16)
            return jnp.dot(pick, feats, preferred_element_type=jnp.float32).astype(jnp.bfloat16)

        most = n_z * unit_rows
        at = jnp.arange(n_pipe * most, dtype=jnp.int32)
        y = (section - at // most) % n_pipe
        feats = features(at // unit_rows % n_z, y, at % rows).reshape(n_pipe, most, CORES * tokens)
        feats = [feats[h] for h in range(n_pipe)]
        sub_of_row = jnp.arange(most, dtype=jnp.int32) // rows % SUB
        sub_mask = (sub_of_row[None, :] == jnp.arange(SUB, dtype=jnp.int32)[:, None]).astype(jnp.bfloat16)
        sub_mask = jnp.broadcast_to(sub_mask[:, :, None], (SUB, most, CORES * tokens))

        view_policy = jnp.dot(policy_out, own.T, preferred_element_type=jnp.float32)
        part_policy = jnp.sum(attn_policy[0].T.astype(jnp.float32) * view_policy, axis=0)
        view_policy = shift(view_policy, -1)

        same_group = (group_ids[:, None] == group_ids[None, :]).astype(jnp.float32)
        group_mean = jnp.dot(same_group, rewards, precision=lax.Precision.HIGHEST) / jnp.sum(same_group, axis=1)
        advantage = rewards - group_mean
        chosen = jnp.arange(rewards.shape[0], dtype=jnp.int32) == lax.axis_index("dp")
        adv_one = jnp.sum(jnp.where(chosen, advantage, 0.0))
        start_one = jnp.sum(jnp.where(chosen, prompt_len, 0))
        length_one = jnp.sum(jnp.where(chosen, response_len, 0))
        seq_total = tokens * n_pipe
        positions = section * tokens + jnp.arange(tokens, dtype=jnp.int32)
        inside = (positions >= start_one) & (positions < start_one + length_one)
        weighting = jnp.where(inside, seq_total / length_one.astype(jnp.float32), 0.0)

        block, other, feats, sub_mask, view_policy, part_policy, weighting, adv_one = lax.optimization_barrier(
            (got_z.reshape(most, step), other, feats, sub_mask, view_policy, part_policy, weighting, adv_one)
        )

        def sums(items):
            return block_sums(items, own, other, sub_mask)

        up, down = block, block
        arrived = [(block, feats[0])]
        parts = []
        for hop in range(1, half):
            up = shift(up, 1)
            down = shift(down, -1)
            if hop > 1:
                parts.append(sums(arrived))
                arrived = []
            arrived += [(up, feats[hop]), (down, feats[n_pipe - hop])]
        cut = most // 2
        last_up = shift(up[:cut], 1)
        last_down = shift(down[cut:], -1)
        parts.append(sums(arrived))
        parts.append(sums([(last_up, feats[half][:cut]), (last_down, feats[half][cut:])]))
        total = sum(parts)[0]

        mine, yours = total[:tokens], total[tokens:]
        zero = jnp.zeros_like(mine)
        same = jnp.stack([mine, part_policy])
        cross = jnp.stack([yours, zero])
        by_core = jnp.where(core == 0, jnp.stack([same, cross]), jnp.stack([cross, same]))
        sent = jnp.broadcast_to(by_core[:, None], (CORES, n_tensor, 2, tokens)).reshape(CORES * n_tensor, 2, tokens)
        gathered = lax.all_to_all(sent, ("dp", "tensor"), 0, 0, axis_index_groups=heads, tiled=True)
        summed = gathered.sum(axis=0)
        logp_frozen = rest_frozen[0] + summed[0]
        logp_policy = rest_policy[0] + summed[1]
        slope = weighting * (KL_WEIGHT * (1.0 - jnp.exp(logp_frozen - logp_policy)) - adv_one)
        slope = shift(slope[None], -1)
        token_grad = (slope * view_policy).astype(jnp.bfloat16)
        return token_grad.T[None]

    return shards


def solution(mesh):
    placed = (
        P("dp", "pipe", "tensor"),
        P("dp", "pipe", "tensor"),
        P("dp", "pipe", None),
        P("dp", "pipe"),
        P("dp", "pipe"),
        P("tensor", None),
        P(("tensor", "dp", "pipe"), None),
        P(),
        P(),
        P(),
        P(),
    )
    return jax.shard_map(
        make(mesh), mesh=mesh, in_specs=placed, out_specs=P("dp", "pipe", "tensor"), check_vma=False
    )
```

```python
import jax
import jax.numpy as jnp
from jax import lax
from jax.experimental import pallas as pl
from jax.experimental.pallas import tpu as pltpu
from jax.sharding import PartitionSpec as P

KL_WEIGHT = 0.1
AXES = ("dp", "tensor", "pipe")
MEMBERS = 4
SUB = 4
MASK_ROWS = 48
STEPS = 2
VMEM_BYTES = 24 * 1024 * 1024


def block_sums(items, feats, seen, sub_mask):
    count = len(items)
    tokens = seen.shape[0]
    step = items[0][0].shape[1]

    def kernel(*refs):
        mask_ref, seen_ref, out_ref = refs[2 * count :]
        total = jnp.zeros((1, tokens), jnp.float32)
        for k in range(SUB // STEPS):
            terms = jnp.zeros((MASK_ROWS, tokens), jnp.float32)
            for row_ref, feat_ref in zip(refs[:count], refs[count : 2 * count]):
                view = lax.dot_general(
                    row_ref[...],
                    seen_ref[:, k * step : (k + 1) * step],
                    (((1,), (1,)), ((), ())),
                    preferred_element_type=jnp.float32,
                )
                for at in range(0, row_ref.shape[0], MASK_ROWS):
                    terms += view[at : at + MASK_ROWS] * feat_ref[0, at : at + MASK_ROWS, :].astype(jnp.float32)
            total += jnp.sum(terms * mask_ref[k].astype(jnp.float32), axis=0, keepdims=True)

        @pl.when(pl.program_id(0) == 0)
        def _():
            out_ref[...] = total

        @pl.when(pl.program_id(0) > 0)
        def _():
            out_ref[...] += total

    blocks = [r for r, _ in items]
    rows = sum(r.shape[0] for r, _ in items)
    specs = [pl.BlockSpec(x.shape, lambda k: (0, 0)) for x in blocks]
    specs += [pl.BlockSpec((1, *feats.shape[1:]), lambda k, at=at: (at, 0, 0)) for _, at in items]
    specs += [
        pl.BlockSpec((SUB // STEPS, MASK_ROWS, tokens), lambda k: (k, 0, 0)),
        pl.BlockSpec((tokens, step * SUB // STEPS), lambda k: (0, k)),
    ]
    return pl.pallas_call(
        kernel,
        grid=(STEPS,),
        out_shape=jax.ShapeDtypeStruct((1, tokens), jnp.float32),
        in_specs=specs,
        out_specs=pl.BlockSpec((1, tokens), lambda k: (0, 0)),
        cost_estimate=pl.CostEstimate(
            flops=2 * rows * SUB * step * tokens, bytes_accessed=rows * step * 2 + 2 * seen.size, transcendentals=0
        ),
        compiler_params=pltpu.CompilerParams(dimension_semantics=("arbitrary",), vmem_limit_bytes=VMEM_BYTES),
    )(*blocks, *[feats] * count, sub_mask, seen)


def column_parts(array, count):
    rows, width = array.shape
    part = width // count

    def kernel(in_ref, out_ref):
        out_ref[0] = in_ref[...]

    return pl.pallas_call(
        kernel,
        grid=(count,),
        out_shape=jax.ShapeDtypeStruct((count, rows, part), array.dtype),
        in_specs=[pl.BlockSpec((rows, part), lambda m: (0, m))],
        out_specs=pl.BlockSpec((1, rows, part), lambda m: (m, 0, 0)),
        cost_estimate=pl.CostEstimate(flops=0, bytes_accessed=4 * array.size, transcendentals=0),
        compiler_params=pltpu.CompilerParams(dimension_semantics=("arbitrary",), vmem_limit_bytes=VMEM_BYTES),
    )(array)


def in_hbm(array):
    return pltpu.with_memory_space_constraint(array, pltpu.HBM)


def make(mesh):
    n_dp, n_tensor, n_pipe = (mesh.shape[a] for a in AXES)
    half = n_pipe // 2
    groups = [list(range(lo, lo + MEMBERS)) for lo in range(0, n_dp, MEMBERS)]
    heads = [[d * n_tensor + t for d in group for t in range(n_tensor)] for group in groups]

    def shift(array, by):
        return lax.ppermute(array, "pipe", [(i, (i + by) % n_pipe) for i in range(n_pipe)])

    def shards(
        attn_policy,
        attn_frozen,
        readout,
        rest_policy,
        rest_frozen,
        policy_out,
        frozen_out,
        rewards,
        group_ids,
        prompt_len,
        response_len,
    ):
        own = readout[0]
        tokens, width = own.shape
        rows = frozen_out.shape[0]
        quarter = width // MEMBERS
        step = quarter // SUB
        member = lax.axis_index("dp") % MEMBERS
        section = lax.axis_index("pipe")
        unit_rows = SUB * rows
        block_rows = n_dp * unit_rows
        shared = MEMBERS * tokens

        parts = frozen_out.reshape(rows, MEMBERS, SUB, step).transpose(1, 2, 0, 3).reshape(MEMBERS, unit_rows, step)
        parts = jnp.broadcast_to(parts[None], (n_dp // MEMBERS, MEMBERS, unit_rows, step))
        block = lax.all_to_all(parts.reshape(n_dp, unit_rows, step), "dp", 0, 0, tiled=True)
        block = block.reshape(block_rows, step)

        split = column_parts(own, MEMBERS)
        seen = lax.all_to_all(split, "dp", 0, 0, axis_index_groups=groups, tiled=True).reshape(shared, quarter)
        seen = in_hbm(seen)

        view_policy = jnp.dot(policy_out, own.T, preferred_element_type=jnp.float32)
        part_policy = jnp.sum(attn_policy[0].T.astype(jnp.float32) * view_policy, axis=0)

        feats = attn_frozen[0].T
        for bit in (1, 2):
            theirs = lax.ppermute(feats, "dp", [(d, d ^ bit) for d in range(n_dp)])
            if bit == 2:
                block, view_policy, part_policy, theirs = lax.optimization_barrier(
                    (block, view_policy, part_policy, theirs)
                )
            second = (member & bit) != 0
            feats = jnp.concatenate(
                [jnp.where(second, theirs, feats), jnp.where(second, feats, theirs)], axis=1
            )
        at = jnp.arange(n_pipe * block_rows, dtype=jnp.int32)
        source = at // unit_rows % n_dp * n_pipe + (section - at // block_rows) % n_pipe
        source = source * rows + at % rows
        columns = jnp.arange(n_dp * n_pipe * rows, dtype=jnp.int32)
        pick = (source[:, None] == columns[None, :]).astype(jnp.bfloat16)
        feats = jnp.dot(pick, feats, preferred_element_type=jnp.float32).astype(jnp.bfloat16)
        feats = in_hbm(feats.reshape(n_pipe, block_rows, shared))
        sub_of_row = jnp.arange(MASK_ROWS, dtype=jnp.int32) // rows % SUB
        sub_mask = (sub_of_row[None, :] == jnp.arange(SUB, dtype=jnp.int32)[:, None]).astype(jnp.bfloat16)
        sub_mask = jnp.broadcast_to(sub_mask[:, :, None], (SUB, MASK_ROWS, shared))

        def sums(items):
            return block_sums(items, feats, seen, sub_mask)

        up, down = block, block
        arrived = [[(block, 0)]]
        for hop in range(1, half):
            up = shift(up, 1)
            down = shift(down, -1)
            arrived.append([(up, hop), (down, n_pipe - hop)])
        last = shift(up, 1)
        total = sums(arrived[0] + arrived[1] + arrived[2] + arrived[3])
        total += sums([(last, half)])

        frozen = total.reshape(MEMBERS, 1, tokens)
        me = jnp.arange(MEMBERS, dtype=jnp.int32)[:, None, None] == member
        policy = jnp.where(me, part_policy[None, None, :], 0.0)
        sent = jnp.concatenate([frozen, policy], axis=1)
        sent = jnp.broadcast_to(sent[:, None], (MEMBERS, n_tensor, 2, tokens)).reshape(MEMBERS * n_tensor, 2, tokens)
        sent, rewards, group_ids, prompt_len, response_len = lax.optimization_barrier(
            (sent, rewards, group_ids, prompt_len, response_len)
        )
        gathered = lax.all_to_all(sent, ("dp", "tensor"), 0, 0, axis_index_groups=heads, tiled=True)
        summed = gathered.sum(axis=0)

        same_group = (group_ids[:, None] == group_ids[None, :]).astype(jnp.float32)
        group_mean = jnp.dot(same_group, rewards, precision=lax.Precision.HIGHEST) / jnp.sum(same_group, axis=1)
        advantage = rewards - group_mean
        chosen = jnp.arange(rewards.shape[0], dtype=jnp.int32) == lax.axis_index("dp")
        adv_one = jnp.sum(jnp.where(chosen, advantage, 0.0))
        start_one = jnp.sum(jnp.where(chosen, prompt_len, 0))
        length_one = jnp.sum(jnp.where(chosen, response_len, 0))
        seq_total = tokens * n_pipe
        positions = section * tokens + jnp.arange(tokens, dtype=jnp.int32)
        inside = (positions >= start_one) & (positions < start_one + length_one)
        weighting = jnp.where(inside, seq_total / length_one.astype(jnp.float32), 0.0)

        logp_frozen = rest_frozen[0] + summed[0]
        logp_policy = rest_policy[0] + summed[1]
        slope = weighting * (KL_WEIGHT * (1.0 - jnp.exp(logp_frozen - logp_policy)) - adv_one)
        view_policy = shift(view_policy, -1)
        slope = shift(slope[None], -1)
        token_grad = (slope * view_policy).astype(jnp.bfloat16)
        return token_grad.T[None]

    return shards


def solution(mesh):
    placed = (
        P("dp", "pipe", "tensor"),
        P("dp", "pipe", "tensor"),
        P("dp", "pipe", None),
        P("dp", "pipe"),
        P("dp", "pipe"),
        P("tensor", None),
        P(("tensor", "dp", "pipe"), None),
        P(),
        P(),
        P(),
        P(),
    )
    return jax.shard_map(
        make(mesh), mesh=mesh, in_specs=placed, out_specs=P("dp", "pipe", "tensor"), check_vma=False
    )
```

```python
import jax
import jax.numpy as jnp
from jax import lax
from jax.experimental import pallas as pl
from jax.experimental.pallas import tpu as pltpu
from jax.sharding import PartitionSpec as P

KL_WEIGHT = 0.1
AXES = ("dp", "tensor", "pipe")
MEMBERS = 4
SUB = 4
MASK_ROWS = 48
STEPS = 2
VMEM_BYTES = 24 * 1024 * 1024


def block_sums(items, feats, seen, sub_mask):
    count = len(items)
    tokens = seen.shape[0]
    step = items[0][0].shape[1]

    def kernel(*refs):
        mask_ref, seen_ref, out_ref = refs[2 * count :]
        total = jnp.zeros((1, tokens), jnp.float32)
        for k in range(SUB // STEPS):
            terms = jnp.zeros((MASK_ROWS, tokens), jnp.float32)
            for row_ref, feat_ref in zip(refs[:count], refs[count : 2 * count]):
                view = lax.dot_general(
                    row_ref[...],
                    seen_ref[:, k * step : (k + 1) * step],
                    (((1,), (1,)), ((), ())),
                    preferred_element_type=jnp.float32,
                )
                for at in range(0, row_ref.shape[0], MASK_ROWS):
                    terms += view[at : at + MASK_ROWS] * feat_ref[0, at : at + MASK_ROWS, :].astype(jnp.float32)
            total += jnp.sum(terms * mask_ref[k].astype(jnp.float32), axis=0, keepdims=True)

        @pl.when(pl.program_id(0) == 0)
        def _():
            out_ref[...] = total

        @pl.when(pl.program_id(0) > 0)
        def _():
            out_ref[...] += total

    blocks = [r for r, _ in items]
    rows = sum(r.shape[0] for r, _ in items)
    specs = [pl.BlockSpec(x.shape, lambda k: (0, 0)) for x in blocks]
    specs += [pl.BlockSpec((1, *feats.shape[1:]), lambda k, at=at: (at, 0, 0)) for _, at in items]
    specs += [
        pl.BlockSpec((SUB // STEPS, MASK_ROWS, tokens), lambda k: (k, 0, 0)),
        pl.BlockSpec((tokens, step * SUB // STEPS), lambda k: (0, k)),
    ]
    return pl.pallas_call(
        kernel,
        grid=(STEPS,),
        out_shape=jax.ShapeDtypeStruct((1, tokens), jnp.float32),
        in_specs=specs,
        out_specs=pl.BlockSpec((1, tokens), lambda k: (0, 0)),
        cost_estimate=pl.CostEstimate(
            flops=2 * rows * SUB * step * tokens, bytes_accessed=rows * step * 2 + 2 * seen.size, transcendentals=0
        ),
        compiler_params=pltpu.CompilerParams(dimension_semantics=("arbitrary",), vmem_limit_bytes=VMEM_BYTES),
    )(*blocks, *[feats] * count, sub_mask, seen)


def column_parts(array, count):
    rows, width = array.shape
    part = width // count

    def kernel(in_ref, out_ref):
        out_ref[0] = in_ref[...]

    return pl.pallas_call(
        kernel,
        grid=(count,),
        out_shape=jax.ShapeDtypeStruct((count, rows, part), array.dtype),
        in_specs=[pl.BlockSpec((rows, part), lambda m: (0, m))],
        out_specs=pl.BlockSpec((1, rows, part), lambda m: (m, 0, 0)),
        cost_estimate=pl.CostEstimate(flops=0, bytes_accessed=4 * array.size, transcendentals=0),
        compiler_params=pltpu.CompilerParams(dimension_semantics=("arbitrary",), vmem_limit_bytes=VMEM_BYTES),
    )(array)


def in_hbm(array):
    return pltpu.with_memory_space_constraint(array, pltpu.HBM)


def make(mesh):
    n_dp, n_tensor, n_pipe = (mesh.shape[a] for a in AXES)
    half = n_pipe // 2
    groups = [list(range(lo, lo + MEMBERS)) for lo in range(0, n_dp, MEMBERS)]
    heads = [[d * n_tensor + t for d in group for t in range(n_tensor)] for group in groups]

    def shift(array, by):
        return lax.ppermute(array, "pipe", [(i, (i + by) % n_pipe) for i in range(n_pipe)])

    def shards(
        attn_policy,
        attn_frozen,
        readout,
        rest_policy,
        rest_frozen,
        policy_out,
        frozen_out,
        rewards,
        group_ids,
        prompt_len,
        response_len,
    ):
        own = readout[0]
        tokens, width = own.shape
        rows = frozen_out.shape[0]
        quarter = width // MEMBERS
        step = quarter // SUB
        member = lax.axis_index("dp") % MEMBERS
        section = lax.axis_index("pipe")
        unit_rows = SUB * rows
        block_rows = n_dp * unit_rows
        shared = MEMBERS * tokens

        parts = frozen_out.reshape(rows, MEMBERS, SUB, step).transpose(1, 2, 0, 3).reshape(MEMBERS, unit_rows, step)
        parts = jnp.broadcast_to(parts[None], (n_dp // MEMBERS, MEMBERS, unit_rows, step))
        block = lax.all_to_all(parts.reshape(n_dp, unit_rows, step), "dp", 0, 0, tiled=True)
        block = block.reshape(block_rows, step)

        split = column_parts(own, MEMBERS)
        seen = lax.all_to_all(split, "dp", 0, 0, axis_index_groups=groups, tiled=True).reshape(shared, quarter)
        seen = in_hbm(seen)

        view_policy = jnp.dot(policy_out, own.T, preferred_element_type=jnp.float32)
        part_policy = jnp.sum(attn_policy[0].T.astype(jnp.float32) * view_policy, axis=0)

        feats = attn_frozen[0].T
        for bit in (1, 2):
            theirs = lax.ppermute(feats, "dp", [(d, d ^ bit) for d in range(n_dp)])
            second = (member & bit) != 0
            feats = jnp.concatenate(
                [jnp.where(second, theirs, feats), jnp.where(second, feats, theirs)], axis=1
            )
        at = jnp.arange(n_pipe * block_rows, dtype=jnp.int32)
        source = at // unit_rows % n_dp * n_pipe + (section - at // block_rows) % n_pipe
        source = source * rows + at % rows
        columns = jnp.arange(n_dp * n_pipe * rows, dtype=jnp.int32)
        pick = (source[:, None] == columns[None, :]).astype(jnp.bfloat16)
        feats = jnp.dot(pick, feats, preferred_element_type=jnp.float32).astype(jnp.bfloat16)
        feats = in_hbm(feats.reshape(n_pipe, block_rows, shared))
        sub_of_row = jnp.arange(MASK_ROWS, dtype=jnp.int32) // rows % SUB
        sub_mask = (sub_of_row[None, :] == jnp.arange(SUB, dtype=jnp.int32)[:, None]).astype(jnp.bfloat16)
        sub_mask = jnp.broadcast_to(sub_mask[:, :, None], (SUB, MASK_ROWS, shared))

        block, view_policy, part_policy = lax.optimization_barrier((block, view_policy, part_policy))

        def sums(items):
            return block_sums(items, feats, seen, sub_mask)

        def statistics(rewards, group_ids, prompt_len, response_len):
            same_group = (group_ids[:, None] == group_ids[None, :]).astype(jnp.float32)
            group_mean = jnp.dot(same_group, rewards, precision=lax.Precision.HIGHEST) / jnp.sum(same_group, axis=1)
            advantage = rewards - group_mean
            chosen = jnp.arange(rewards.shape[0], dtype=jnp.int32) == lax.axis_index("dp")
            adv_one = jnp.sum(jnp.where(chosen, advantage, 0.0))
            start_one = jnp.sum(jnp.where(chosen, prompt_len, 0))
            length_one = jnp.sum(jnp.where(chosen, response_len, 0))
            seq_total = tokens * n_pipe
            positions = section * tokens + jnp.arange(tokens, dtype=jnp.int32)
            inside = (positions >= start_one) & (positions < start_one + length_one)
            weighting = jnp.where(inside, seq_total / length_one.astype(jnp.float32), 0.0)
            return weighting, adv_one

        up, down = block, block
        arrived = [[(block, 0)]]
        for hop in range(1, half):
            up = shift(up, 1)
            down = shift(down, -1)
            arrived.append([(up, hop), (down, n_pipe - hop)])
        last = shift(up, 1)
        total = sums(arrived[0] + arrived[1] + arrived[2])
        total += sums(arrived[3] + [(last, half)])

        frozen = total.reshape(MEMBERS, 1, tokens)
        me = jnp.arange(MEMBERS, dtype=jnp.int32)[:, None, None] == member
        policy = jnp.where(me, part_policy[None, None, :], 0.0)
        sent = jnp.concatenate([frozen, policy], axis=1)
        sent = jnp.broadcast_to(sent[:, None], (MEMBERS, n_tensor, 2, tokens)).reshape(MEMBERS * n_tensor, 2, tokens)
        sent, *group = lax.optimization_barrier((sent, rewards, group_ids, prompt_len, response_len))
        gathered = lax.all_to_all(sent, ("dp", "tensor"), 0, 0, axis_index_groups=heads, tiled=True)
        summed = gathered.sum(axis=0)

        weighting, adv_one = statistics(*group)
        logp_frozen = rest_frozen[0] + summed[0]
        logp_policy = rest_policy[0] + summed[1]
        slope = weighting * (KL_WEIGHT * (1.0 - jnp.exp(logp_frozen - logp_policy)) - adv_one)
        view_policy = shift(view_policy, -1)
        slope = shift(slope[None], -1)
        token_grad = (slope * view_policy).astype(jnp.bfloat16)
        return token_grad.T[None]

    return shards


def solution(mesh):
    placed = (
        P("dp", "pipe", "tensor"),
        P("dp", "pipe", "tensor"),
        P("dp", "pipe", None),
        P("dp", "pipe"),
        P("dp", "pipe"),
        P("tensor", None),
        P(("tensor", "dp", "pipe"), None),
        P(),
        P(),
        P(),
        P(),
    )
    return jax.shard_map(
        make(mesh), mesh=mesh, in_specs=placed, out_specs=P("dp", "pipe", "tensor"), check_vma=False
    )
```

```python
import jax
import jax.numpy as jnp
from jax import lax
from jax.experimental import pallas as pl
from jax.experimental.pallas import tpu as pltpu
from jax.sharding import PartitionSpec as P

KL_WEIGHT = 0.1
AXES = ("dp", "tensor", "pipe")
MEMBERS = 4
SUB = 4
STEPS = 2
VMEM_BYTES = 24 * 1024 * 1024


def block_sums(items, feats, seen):
    count = len(items)
    tokens = seen.shape[0]
    step = items[0][0].shape[1]
    n = feats.shape[1]

    def kernel(*refs):
        seen_ref, out_ref = refs[2 * count :]
        first = pl.program_id(0) * (SUB // STEPS)
        view = jnp.zeros((count * n, tokens), jnp.float32)
        for k in range(SUB // STEPS):
            part = pl.ds(pl.multiple_of((first + k) * n, 8), n)
            view += lax.dot_general(
                jnp.concatenate([r[part, :] for r in refs[:count]], axis=0),
                seen_ref[:, k * step : (k + 1) * step],
                (((1,), (1,)), ((), ())),
                preferred_element_type=jnp.float32,
            )
        total = jnp.zeros((1, tokens), jnp.float32)
        for i, feat_ref in enumerate(refs[count : 2 * count]):
            terms = view[i * n : (i + 1) * n] * feat_ref[0].astype(jnp.float32)
            total += jnp.sum(terms, axis=0, keepdims=True)

        @pl.when(pl.program_id(0) == 0)
        def _():
            out_ref[...] = total

        @pl.when(pl.program_id(0) > 0)
        def _():
            out_ref[...] += total

    blocks = [r for r, _ in items]
    rows = sum(r.shape[0] for r, _ in items)
    specs = [pl.BlockSpec(x.shape, lambda k: (0, 0)) for x in blocks]
    specs += [pl.BlockSpec((1, *feats.shape[1:]), lambda k, at=at: (at, 0, 0)) for _, at in items]
    specs += [
        pl.BlockSpec((tokens, step * SUB // STEPS), lambda k: (0, k)),
    ]
    return pl.pallas_call(
        kernel,
        grid=(STEPS,),
        out_shape=jax.ShapeDtypeStruct((1, tokens), jnp.float32),
        in_specs=specs,
        out_specs=pl.BlockSpec((1, tokens), lambda k: (0, 0)),
        cost_estimate=pl.CostEstimate(
            flops=2 * rows * SUB * step * tokens, bytes_accessed=rows * step * 2 + 2 * seen.size, transcendentals=0
        ),
        compiler_params=pltpu.CompilerParams(dimension_semantics=("arbitrary",), vmem_limit_bytes=VMEM_BYTES),
    )(*blocks, *[feats] * count, seen)


def column_parts(array, count):
    rows, width = array.shape
    part = width // count

    def kernel(in_ref, out_ref):
        out_ref[0] = in_ref[...]

    return pl.pallas_call(
        kernel,
        grid=(count,),
        out_shape=jax.ShapeDtypeStruct((count, rows, part), array.dtype),
        in_specs=[pl.BlockSpec((rows, part), lambda m: (0, m))],
        out_specs=pl.BlockSpec((1, rows, part), lambda m: (m, 0, 0)),
        cost_estimate=pl.CostEstimate(flops=0, bytes_accessed=4 * array.size, transcendentals=0),
        compiler_params=pltpu.CompilerParams(dimension_semantics=("arbitrary",), vmem_limit_bytes=VMEM_BYTES),
    )(array)


def in_hbm(array):
    return pltpu.with_memory_space_constraint(array, pltpu.HBM)


def make(mesh):
    n_dp, n_tensor, n_pipe = (mesh.shape[a] for a in AXES)
    half = n_pipe // 2
    groups = [list(range(lo, lo + MEMBERS)) for lo in range(0, n_dp, MEMBERS)]
    heads = [[d * n_tensor + t for d in group for t in range(n_tensor)] for group in groups]

    def shift(array, by):
        return lax.ppermute(array, "pipe", [(i, (i + by) % n_pipe) for i in range(n_pipe)])

    def shards(
        attn_policy,
        attn_frozen,
        readout,
        rest_policy,
        rest_frozen,
        policy_out,
        frozen_out,
        rewards,
        group_ids,
        prompt_len,
        response_len,
    ):
        own = readout[0]
        tokens, width = own.shape
        rows = frozen_out.shape[0]
        quarter = width // MEMBERS
        step = quarter // SUB
        member = lax.axis_index("dp") % MEMBERS
        section = lax.axis_index("pipe")
        unit_rows = SUB * rows
        block_rows = n_dp * unit_rows
        shared = MEMBERS * tokens

        parts = frozen_out.reshape(rows, MEMBERS, SUB, step).transpose(1, 2, 0, 3).reshape(MEMBERS, unit_rows, step)
        parts = jnp.broadcast_to(parts[None], (n_dp // MEMBERS, MEMBERS, unit_rows, step))
        block = lax.all_to_all(parts.reshape(n_dp, unit_rows, step), "dp", 0, 0, tiled=True)
        at = jnp.arange(block_rows, dtype=jnp.int32)
        source = at // rows % n_dp * unit_rows + at // (n_dp * rows) * rows + at % rows
        order = (source[:, None] == at[None, :]).astype(jnp.bfloat16)
        block = jnp.dot(order, block.reshape(block_rows, step), preferred_element_type=jnp.float32)
        block = block.astype(jnp.bfloat16)

        split = column_parts(own, MEMBERS)
        seen = lax.all_to_all(split, "dp", 0, 0, axis_index_groups=groups, tiled=True).reshape(shared, quarter)
        seen = in_hbm(seen)

        view_policy = jnp.dot(policy_out, own.T, preferred_element_type=jnp.float32)
        part_policy = jnp.sum(attn_policy[0].T.astype(jnp.float32) * view_policy, axis=0)

        feats = attn_frozen[0].T
        for bit in (1, 2):
            theirs = lax.ppermute(feats, "dp", [(d, d ^ bit) for d in range(n_dp)])
            second = (member & bit) != 0
            feats = jnp.concatenate(
                [jnp.where(second, theirs, feats), jnp.where(second, feats, theirs)], axis=1
            )
        at = jnp.arange(n_pipe * n_dp * rows, dtype=jnp.int32)
        source = at // rows % n_dp * n_pipe + (section - at // (n_dp * rows)) % n_pipe
        source = source * rows + at % rows
        columns = jnp.arange(n_dp * n_pipe * rows, dtype=jnp.int32)
        pick = (source[:, None] == columns[None, :]).astype(jnp.bfloat16)
        feats = jnp.dot(pick, feats, preferred_element_type=jnp.float32).astype(jnp.bfloat16)
        feats = in_hbm(feats.reshape(n_pipe, n_dp * rows, shared))

        block, view_policy, part_policy = lax.optimization_barrier((block, view_policy, part_policy))

        def sums(items):
            return block_sums(items, feats, seen)

        def statistics(rewards, group_ids, prompt_len, response_len):
            same_group = (group_ids[:, None] == group_ids[None, :]).astype(jnp.float32)
            group_mean = jnp.dot(same_group, rewards, precision=lax.Precision.HIGHEST) / jnp.sum(same_group, axis=1)
            advantage = rewards - group_mean
            chosen = jnp.arange(rewards.shape[0], dtype=jnp.int32) == lax.axis_index("dp")
            adv_one = jnp.sum(jnp.where(chosen, advantage, 0.0))
            start_one = jnp.sum(jnp.where(chosen, prompt_len, 0))
            length_one = jnp.sum(jnp.where(chosen, response_len, 0))
            seq_total = tokens * n_pipe
            positions = section * tokens + jnp.arange(tokens, dtype=jnp.int32)
            inside = (positions >= start_one) & (positions < start_one + length_one)
            weighting = jnp.where(inside, seq_total / length_one.astype(jnp.float32), 0.0)
            return weighting, adv_one

        up, down = block, block
        arrived = [[(block, 0)]]
        for hop in range(1, half):
            up = shift(up, 1)
            down = shift(down, -1)
            arrived.append([(up, hop), (down, n_pipe - hop)])
        last = shift(up, 1)
        total = sums(arrived[0] + arrived[1] + arrived[2] + arrived[3])
        total += sums([(last, half)])

        frozen = total.reshape(MEMBERS, 1, tokens)
        me = jnp.arange(MEMBERS, dtype=jnp.int32)[:, None, None] == member
        policy = jnp.where(me, part_policy[None, None, :], 0.0)
        sent = jnp.concatenate([frozen, policy], axis=1)
        sent = jnp.broadcast_to(sent[:, None], (MEMBERS, n_tensor, 2, tokens)).reshape(MEMBERS * n_tensor, 2, tokens)
        sent, *group = lax.optimization_barrier((sent, rewards, group_ids, prompt_len, response_len))
        gathered = lax.all_to_all(sent, ("dp", "tensor"), 0, 0, axis_index_groups=heads, tiled=True)
        summed = gathered.sum(axis=0)

        weighting, adv_one = statistics(*group)
        logp_frozen = rest_frozen[0] + summed[0]
        logp_policy = rest_policy[0] + summed[1]
        slope = weighting * (KL_WEIGHT * (1.0 - jnp.exp(logp_frozen - logp_policy)) - adv_one)
        view_policy = shift(view_policy, -1)
        slope = shift(slope[None], -1)
        token_grad = (slope * view_policy).astype(jnp.bfloat16)
        return token_grad.T[None]

    return shards


def solution(mesh):
    placed = (
        P("dp", "pipe", "tensor"),
        P("dp", "pipe", "tensor"),
        P("dp", "pipe", None),
        P("dp", "pipe"),
        P("dp", "pipe"),
        P("tensor", None),
        P(("tensor", "dp", "pipe"), None),
        P(),
        P(),
        P(),
        P(),
    )
    return jax.shard_map(
        make(mesh), mesh=mesh, in_specs=placed, out_specs=P("dp", "pipe", "tensor"), check_vma=False
    )
```
